512 devices in a mesh: dp: 16 (over x_lo, y, core), ctx: 32 (over z, x_hi).
Axes of the slice: x: 4 (x_hi: 2, x_lo: 2; x = x_hi * 2 + x_lo), y: 4, z: 16, core: 2. Of those that a mesh axis runs over, the one named last changes fastest.
Arguments:
- span_ids: int32 [16, 64], P('dp'), may hold values from 0 to 63, as said below
- hidden_in: bfloat16 [16, 4096, 4096], P('dp', 'ctx'), may hold values from -6 to 6
- queries: bfloat16 [16, 4096, 2048], P('dp', 'ctx'), may hold values from -64 to 64
- keys_in: bfloat16 [16, 4096, 512], P('dp', 'ctx'), may hold values from -4 to 4
- values_in: bfloat16 [16, 4096, 512], P('dp', 'ctx'), may hold values from -4 to 4
- attn_out: bfloat16 [16, 4096, 2048], P('dp', 'ctx'), may hold values from -4 to 4, as said below
- out_grad: bfloat16 [16, 4096, 2048], P('dp', 'ctx'), may hold values from -6 to 6
- log_norm: float32 [16, 4096, 16], P('dp', 'ctx'), may hold values from -300 to 3000, as said below
- adapter: float32 [8, 5120], P(None, 'dp'), may hold values from -0.3 to 0.3
- moment_first: float32 [8, 5120], P(None, 'dp'), may hold values from -0.0078125 to 0.0078125
- moment_second: float32 [8, 5120], P(None, 'dp'), may hold values from 6.103516e-08 to 9.765625e-07
Outputs:
- query_grad: bfloat16 [16, 4096, 2048], P('dp', 'ctx')
- kv_grad: bfloat16 [16, 4096, 1024], P('dp', 'ctx')
- adapter_step: float32 [8, 5120], P(None, 'dp')
The draws below stay inside these ranges and needn't reach their ends.
Inputs may be any that keep to these rules, and one draw needn't show every extreme that they name: `span_ids`: in each sequence the entries 2c and 2c + 1 belong to device c of ctx; entry 2c + 1 equals 63 minus entry 2c, and the entries 2c over all c are a permutation of 0 to 31, drawn afresh for every sequence. `attn_out`: the saved softmax output of queries, keys_in and values_in under the causal mask by pos. `log_norm`: the log of the causal softmax total of each query row and head.
All inputs are finite; a program needn't handle non-finite values.
Results may differ from the reference program's by a relative error of at most 0.017.
Values may be sent and summed in bfloat16 or wider, within the bound.
No kernel may reach another device: no remote copies, remote signals or barrier semaphores. Data moves between devices by JAX's collectives and lax.ppermute only.
A program may use at most 128 MiB of HBM per device.

```python
import math
import jax
import jax.numpy as jnp
from jax import lax

D = 4096
H = 16
KVH = 4
DH = 128
RANK = 8
ROWS = 128
HALF = 64
LENGTH = 4096
SPANS = 64
SEQS = 16
ADAPT = 5120
N_CTX = 32


def span_table(key):
    seq_keys = jax.random.split(jax.random.fold_in(key, 101), SEQS)
    order = jax.vmap(lambda seq_key: jax.random.permutation(seq_key, N_CTX))(seq_keys).astype(jnp.int32)
    paired = jnp.stack([order, 2 * N_CTX - 1 - order], axis=-1)
    return paired.reshape(SEQS, SPANS).astype(jnp.int32)


def attention_base(key):
    assignment = span_table(key)
    query_base = jax.random.truncated_normal(jax.random.fold_in(key, 202), -4.0, 4.0, (SEQS, LENGTH, H, DH), jnp.float32)
    key_base = jax.random.truncated_normal(jax.random.fold_in(key, 203), -4.0, 4.0, (SEQS, LENGTH, KVH, DH), jnp.float32)
    value_base = jax.random.truncated_normal(jax.random.fold_in(key, 204), -4.0, 4.0, (SEQS, LENGTH, KVH, DH), jnp.float32)
    queries = query_base.reshape(SEQS, LENGTH, H * DH).astype(jnp.bfloat16)
    keys_low = key_base.reshape(SEQS, LENGTH, KVH * DH).astype(jnp.bfloat16)
    values_low = value_base.reshape(SEQS, LENGTH, KVH * DH).astype(jnp.bfloat16)
    return (assignment, queries, keys_low, values_low)


def sequence_stats(seq_args):
    assignment, query_seq, key_seq, value_seq = seq_args
    row_slots = jnp.arange(LENGTH, dtype=jnp.int32)
    positions = assignment[row_slots // HALF] * HALF + row_slots % HALF
    key_heads = key_seq.reshape(LENGTH, KVH, DH).astype(jnp.float32)
    value_heads = value_seq.reshape(LENGTH, KVH, DH).astype(jnp.float32)
    block_rows = min(256, LENGTH)

    def block_stats(block_idx):
        first_row = block_idx * block_rows
        query_rows = lax.dynamic_slice_in_dim(query_seq, first_row, block_rows).reshape(block_rows, KVH, H // KVH, DH).astype(jnp.float32)
        pos_query = lax.dynamic_slice_in_dim(positions, first_row, block_rows)
        scores = jnp.einsum('rkgd,skd->kgrs', query_rows, key_heads) * DH ** (-0.5)
        visible = positions[None, :] <= pos_query[:, None]
        scores = jnp.where(visible, scores, -1e+30)
        row_top = jnp.max(scores, axis=-1, keepdims=True)
        weights = jnp.exp(scores - row_top)
        row_total = jnp.sum(weights, axis=-1, keepdims=True)
        row_norm = row_top[..., 0] + jnp.log(row_total[..., 0])
        outputs = jnp.einsum('kgrs,skd->rkgd', weights / row_total, value_heads)
        return (jnp.transpose(row_norm, (2, 0, 1)).reshape(block_rows, H), outputs.reshape(block_rows, H * DH))
    norms, outputs = lax.map(block_stats, jnp.arange(LENGTH // block_rows, dtype=jnp.int32))
    return (norms.reshape(LENGTH, H), outputs.reshape(LENGTH, H * DH).astype(jnp.bfloat16))


def attention_stats(key):
    assignment, queries, keys_low, values_low = attention_base(key)
    return lax.map(sequence_stats, (assignment, queries, keys_low, values_low))


def draw_span_ids(key, part):
    return span_table(key)


def draw_queries(key, part):
    return attention_base(key)[1]


def draw_keys_in(key, part):
    return attention_base(key)[2]


def draw_values_in(key, part):
    return attention_base(key)[3]


def draw_attn_out(key, part):
    return attention_stats(key)[1]


def draw_log_norm(key, part):
    return attention_stats(key)[0]


def draw_adapter(key, part):
    base = jax.random.truncated_normal(jax.random.fold_in(key, 305), -5.0, 5.0, (RANK, ADAPT), jnp.float32)
    factor = 1.2
    column_iota = jnp.arange(ADAPT, dtype=jnp.int32)
    column_scale = jnp.where(column_iota < D, 0.05 * factor, 0.05 / factor).astype(jnp.float32)
    return jnp.clip(base * column_scale[None, :], -0.3, 0.3).astype(jnp.float32)


def steps_of(rng, shape, shards, least, top_value):
    gain, own = 1.0, jax.random.fold_in(rng, 6)
    for position, blocks in shards:
        heights = jnp.exp(jax.random.uniform(jax.random.fold_in(own, position), (blocks,), jnp.float32, least / len(shards), top_value / len(shards)))
        gain = gain * jnp.repeat(heights, shape[position] // blocks).reshape([-1 if axis == position else 1 for axis in range(len(shape))])
    return gain


def gaussian(own_key, dims, width, limit, pieces=(), kind=jnp.bfloat16):
    array = jax.random.normal(own_key, dims, jnp.float32) * width
    if len(pieces) > 0:
        array = steps_of(own_key, dims, pieces, -0.22, 0.18) * array
    return jnp.clip(array, min=-limit, max=limit).astype(kind)


def setup_inputs(seed: int = 0) -> dict:
    seeds = jax.random.split(jax.random.key(seed), 12)
    return {
        "span_ids": draw_span_ids(jax.random.fold_in(seeds[11], 71), 0),
        "hidden_in": gaussian(seeds[1], (SEQS, LENGTH, D), 1.0, 6.0, ((0, 16), (1, 32))),
        "queries": draw_queries(jax.random.fold_in(seeds[11], 71), 0),
        "keys_in": draw_keys_in(jax.random.fold_in(seeds[11], 71), 0),
        "values_in": draw_values_in(jax.random.fold_in(seeds[11], 71), 0),
        "attn_out": draw_attn_out(jax.random.fold_in(seeds[11], 71), 0),
        "out_grad": gaussian(seeds[6], (SEQS, LENGTH, H * DH), 1.0, 6.0, ((0, 16), (1, 32))),
        "log_norm": draw_log_norm(jax.random.fold_in(seeds[11], 71), 0),
        "adapter": draw_adapter(jax.random.fold_in(seeds[11], 71), 0),
        "moment_first": gaussian(seeds[9], (RANK, ADAPT), (0.1 * (RANK * ADAPT) ** -0.5), 0.0078125, ((1, 16),), jnp.float32),
        "moment_second": jnp.clip(jnp.exp(math.log(9.765625463842298e-07) - 2.7725887 * jax.random.uniform(seeds[10], (RANK, ADAPT), jnp.float32) ** steps_of(seeds[10], (RANK, ADAPT), ((1, 16),), -0.2, 0.2)), 6.103515914901436e-08, 9.765625463842298e-07),
    }


BIAS_ONE = 1.0 - 0.9 ** 100.0
BIAS_TWO = 1.0 - 0.999 ** 100.0

def rounded(values_f32):
    low = lax.optimization_barrier(values_f32.astype(jnp.bfloat16))
    return low.astype(jnp.float32)

def grouped(rows):
    return rows.reshape(rows.shape[0], KVH, H // KVH, DH).astype(jnp.float32)

def per_head(stat_rows):
    return jnp.transpose(stat_rows.reshape(stat_rows.shape[0], KVH, H // KVH), (1, 2, 0))[..., None]

def sequence_grads(seq_args):
    assignment, query_seq, key_seq, value_seq, out_seq, grad_seq, norm_seq = seq_args
    row_slots = jnp.arange(LENGTH, dtype=jnp.int32)
    positions = assignment[row_slots // HALF] * HALF + row_slots % HALF
    key_heads = key_seq.reshape(LENGTH, KVH, DH).astype(jnp.float32)
    value_heads = value_seq.reshape(LENGTH, KVH, DH).astype(jnp.float32)
    score_scale = DH ** (-0.5)

    def device_step(kv_total, device_idx):
        first_row = device_idx * ROWS
        query_rows = grouped(lax.dynamic_slice_in_dim(query_seq, first_row, ROWS))
        grad_rows = grouped(lax.dynamic_slice_in_dim(grad_seq, first_row, ROWS))
        out_rows = grouped(lax.dynamic_slice_in_dim(out_seq, first_row, ROWS))
        norm_rows = per_head(lax.dynamic_slice_in_dim(norm_seq, first_row, ROWS))
        delta_rows = per_head(lax.optimization_barrier(jnp.sum(grad_rows * out_rows, axis=-1)).reshape(ROWS, H))
        pos_query = lax.dynamic_slice_in_dim(positions, first_row, ROWS)
        visible = positions[None, :] <= pos_query[:, None]
        scores = jnp.einsum('rkgd,skd->kgrs', query_rows, key_heads) * score_scale
        weights = jnp.where(visible, jnp.exp(scores - norm_rows), 0.0)
        weights_low = rounded(weights)
        d_weights = jnp.einsum('rkgd,skd->kgrs', grad_rows, value_heads)
        d_scores = rounded(weights * (d_weights - delta_rows))
        query_part = jnp.einsum('kgrs,skd->rkgd', d_scores, key_heads) * score_scale
        key_part = jnp.einsum('kgrs,rkgd->skd', d_scores, query_rows) * score_scale
        value_part = jnp.einsum('kgrs,rkgd->skd', weights_low, grad_rows)
        kv_part = jnp.concatenate([key_part.reshape(LENGTH, KVH * DH), value_part.reshape(LENGTH, KVH * DH)], axis=1)
        return (kv_total + rounded(kv_part), query_part.reshape(ROWS, H * DH).astype(jnp.bfloat16))
    kv_total, query_blocks = lax.scan(device_step, jnp.zeros((LENGTH, 2 * KVH * DH), jnp.float32), jnp.arange(N_CTX, dtype=jnp.int32))
    return (query_blocks.reshape(LENGTH, H * DH), kv_total.astype(jnp.bfloat16))

def reference(span_ids, hidden_in, queries, keys_in, values_in, attn_out, out_grad, log_norm, adapter, moment_first, moment_second):
    query_grad, kv_grad = lax.map(sequence_grads, (span_ids, queries, keys_in, values_in, attn_out, out_grad, log_norm))
    adapter_low = adapter.astype(jnp.bfloat16)
    down_low = adapter_low[:, :D]
    up_low = adapter_low[:, D:]
    input_rows = hidden_in.reshape(-1, D)
    kv_rows = kv_grad.reshape(-1, 2 * KVH * DH)
    mixed_up = jnp.dot(kv_rows, up_low.T, preferred_element_type=jnp.float32).astype(jnp.bfloat16)
    mixed_down = jnp.dot(input_rows, down_low.T, preferred_element_type=jnp.float32).astype(jnp.bfloat16)
    grad_down = jnp.dot(mixed_up.T, input_rows, preferred_element_type=jnp.float32)
    grad_up = jnp.dot(mixed_down.T, kv_rows, preferred_element_type=jnp.float32)
    grad_whole = jnp.concatenate([grad_down, grad_up], axis=1)
    squares = jnp.sum(grad_whole * grad_whole)
    clip_factor = jnp.minimum(1.0, 1.0 / jnp.sqrt(squares + 1e-06))
    scaled = grad_whole * clip_factor
    moment_new = 0.9 * moment_first + 0.1 * scaled
    second_new = 0.999 * moment_second + 0.001 * scaled * scaled
    adapter_step = moment_new / BIAS_ONE / (jnp.sqrt(second_new / BIAS_TWO) + 1e-08)
    return (query_grad, kv_grad, adapter_step)
```

```python
import jax
import jax.numpy as jnp
from jax import lax
from jax.experimental import pallas as pl
from jax.experimental.pallas import tpu as pltpu
from jax.sharding import Mesh
from jax.sharding import PartitionSpec as P

D = 4096
H = 16
KVH = 4
DH = 128
ROWS = 128
HALF = 64
GROUP = H // KVH
KEY_BLOCK = 256
SCALE = DH ** (-0.5)
CTX = ("ctx_0", "ctx_1")
PAIR = ((0, 1), (1, 0))


BIAS_ONE = 1.0 - 0.9**100.0
BIAS_TWO = 1.0 - 0.999**100.0


def prepare_kernel(q_mine, g_mine, q_other, g_other, q_out, g_out, qt_out, gt_out):
    halves = ROWS // HALF
    for j in range(KVH):
        for s in range(2 * halves):
            place = j * 2 * halves + s
            for source, rows_out, cols_out in (
                ((q_mine, q_other)[s // halves], q_out, qt_out),
                ((g_mine, g_other)[s // halves], g_out, gt_out),
            ):
                first = (s % halves) * HALF
                pieces = [
                    source[first : first + HALF, (j * GROUP + g) * DH : (j * GROUP + g + 1) * DH]
                    for g in range(GROUP)
                ]
                rows = jnp.concatenate(pieces, axis=0)
                rows_out[place] = rows
                cols_out[place] = rows.T


def prepared(q_mine, g_mine, q_other, g_other):
    count = KVH * 2 * ROWS // HALF
    vmem = pl.BlockSpec(memory_space=pltpu.VMEM)
    tall = jax.ShapeDtypeStruct((count, GROUP * HALF, DH), jnp.bfloat16)
    wide = jax.ShapeDtypeStruct((count, DH, GROUP * HALF), jnp.bfloat16)
    return pl.pallas_call(
        prepare_kernel,
        out_shape=(tall, tall, wide, wide),
        in_specs=[vmem] * 4,
        out_specs=(vmem,) * 4,
        compiler_params=pltpu.CompilerParams(vmem_limit_bytes=24 * 1024 * 1024),
    )(q_mine, g_mine, q_other, g_other)


def attention_kernel(
    table_ref, kv_ref, q_s, g_s, qt_s, gt_s, stat_ref,
    dq_ref, dkv_ref,
    k_s, v_s, kt_s, dk_s, dv_s, dqt_s,
):
    n_blocks = k_s.shape[1]
    n_spans = q_s.shape[0] // KVH
    pos_at = k_s.shape[1] * (KEY_BLOCK // HALF)
    span_at = 2 * pos_at
    less_at = span_at + n_spans
    seen_at = less_at + n_spans
    per_block = KEY_BLOCK // HALF
    n_rows = GROUP * HALF
    value_at = KVH * DH

    def arrange(b, carry):
        for i in range(per_block):
            row = pl.multiple_of(table_ref[b * per_block + i] * HALF, HALF)
            for j in range(KVH):
                k_s[j, b, pl.ds(i * HALF, HALF), :] = kv_ref[pl.ds(row, HALF), j * DH : (j + 1) * DH]
                v_s[j, b, pl.ds(i * HALF, HALF), :] = kv_ref[
                    pl.ds(row, HALF), value_at + j * DH : value_at + (j + 1) * DH
                ]
        for j in range(KVH):
            kt_s[j, b] = k_s[j, b].T
            dk_s[j, b] = jnp.zeros((KEY_BLOCK, DH), jnp.float32)
            dv_s[j, b] = jnp.zeros((KEY_BLOCK, DH), jnp.float32)
        return carry

    lax.fori_loop(0, n_blocks, arrange, 0)

    def tiles(n, j, s, blocks, masked):
        norm = stat_ref[0, pl.ds(n, 1), :]
        delta = stat_ref[1, pl.ds(n, 1), :]
        low, d_low = [], []
        for b in blocks:
            scores = jnp.dot(k_s[j, b], qt_s[n], preferred_element_type=jnp.float32) * SCALE
            weights = jnp.exp(scores - norm)
            if masked:
                lane = lax.broadcasted_iota(jnp.int32, (HALF, n_rows), 1)
                line = lax.broadcasted_iota(jnp.int32, (HALF, n_rows), 0)
                ahead = line - lax.rem(lane, HALF)
                shifts = [(table_ref[span_at + s] - table_ref[pos_at + b * per_block + i]) * HALF for i in range(per_block)]
                weights = jnp.concatenate(
                    [
                        jnp.where(ahead <= shifts[i], weights[i * HALF : (i + 1) * HALF], 0.0)
                        for i in range(per_block)
                    ],
                    axis=0,
                )
            d_weights = jnp.dot(v_s[j, b], gt_s[n], preferred_element_type=jnp.float32)
            low.append(weights.astype(jnp.bfloat16))
            d_low.append((weights * (d_weights - delta)).astype(jnp.bfloat16))
        total = None
        value_terms = [jnp.dot(w, g_s[n], preferred_element_type=jnp.float32) for w in low]
        key_terms = [jnp.dot(d, q_s[n], preferred_element_type=jnp.float32) for d in d_low]
        for b, d in zip(blocks, d_low):
            term = jnp.dot(kt_s[j, b], d, preferred_element_type=jnp.float32)
            total = term if total is None else total + term
        for b, term in zip(blocks, value_terms):
            dv_s[j, b] += term
        for b, term in zip(blocks, key_terms):
            dk_s[j, b] += term
        dqt_s[...] += total

    def query_span(n, carry):
        j = n // n_spans
        s = lax.rem(n, n_spans)
        whole = table_ref[less_at + s] // per_block
        dqt_s[...] = jnp.zeros(dqt_s.shape, jnp.float32)

        def pair(i, c):
            tiles(n, j, s, (2 * i, 2 * i + 1), False)
            return c

        lax.fori_loop(0, whole // 2, pair, 0)

        @pl.when(lax.rem(whole, 2) == 1)
        def _():
            tiles(n, j, s, (whole - 1,), False)

        @pl.when(table_ref[seen_at + s] > whole * per_block)
        def _():
            tiles(n, j, s, (whole,), True)

        total = (dqt_s[...] * SCALE).T
        row = pl.multiple_of(s * HALF, HALF)
        for g in range(GROUP):
            col = pl.multiple_of((j * GROUP + g) * DH, DH)
            dq_ref[pl.ds(row, HALF), pl.ds(col, DH)] = total[g * HALF : (g + 1) * HALF]
        return carry

    lax.fori_loop(0, KVH * n_spans, query_span, 0)

    def give_back(b, carry):
        for i in range(per_block):
            row = pl.multiple_of(table_ref[b * per_block + i] * HALF, HALF)
            for j in range(KVH):
                rows = pl.ds(i * HALF, HALF)
                dkv_ref[pl.ds(row, HALF), j * DH : (j + 1) * DH] = (dk_s[j, b, rows, :] * SCALE).astype(jnp.bfloat16)
                dkv_ref[pl.ds(row, HALF), value_at + j * DH : value_at + (j + 1) * DH] = dv_s[j, b, rows, :].astype(
                    jnp.bfloat16
                )
        return carry

    lax.fori_loop(0, n_blocks, give_back, 0)


def attention_terms(table, kv, prepared_rows, stats):
    length = kv.shape[0]
    n_blocks = length // KEY_BLOCK
    n_spans = prepared_rows[0].shape[0] // KVH
    smem = pl.BlockSpec(memory_space=pltpu.SMEM)
    vmem = pl.BlockSpec(memory_space=pltpu.VMEM)
    bf, f32 = jnp.bfloat16, jnp.float32
    return pl.pallas_call(
        attention_kernel,
        out_shape=(
            jax.ShapeDtypeStruct((n_spans * HALF, H * DH), f32),
            jax.ShapeDtypeStruct(kv.shape, bf),
        ),
        in_specs=[smem] + [vmem] * 6,
        out_specs=(vmem, vmem),
        scratch_shapes=[
            pltpu.VMEM((KVH, n_blocks, KEY_BLOCK, DH), bf),
            pltpu.VMEM((KVH, n_blocks, KEY_BLOCK, DH), bf),
            pltpu.VMEM((KVH, n_blocks, DH, KEY_BLOCK), bf),
            pltpu.VMEM((KVH, n_blocks, KEY_BLOCK, DH), f32),
            pltpu.VMEM((KVH, n_blocks, KEY_BLOCK, DH), f32),
            pltpu.VMEM((DH, GROUP * HALF), f32),
        ],
        compiler_params=pltpu.CompilerParams(vmem_limit_bytes=30 * 1024 * 1024),
    )(table, kv, *prepared_rows, stats)


def from_everyone(shard, axis):
    count = lax.axis_size(axis)
    return lax.all_to_all(
        jnp.broadcast_to(shard[None], (count, *shard.shape)), axis, 0, 0, tiled=True
    )


def swapped(block):
    return lax.ppermute(block, "ctx_1", PAIR)


def stat_rows(stats):
    tall = stats.reshape(ROWS // HALF, HALF, KVH, GROUP)
    return jnp.transpose(tall, (2, 0, 3, 1)).reshape(KVH, ROWS // HALF, GROUP * HALF)


def span_tables(span_ids):
    me_x = lax.axis_index("ctx_1")
    places = span_ids.reshape(lax.axis_size("ctx_0"), 2, ROWS // HALF)
    key_spans = lax.dynamic_index_in_dim(places, me_x, 1, keepdims=False).reshape(-1)
    here = lax.dynamic_index_in_dim(places, lax.axis_index("ctx_0"), 0, keepdims=False)
    own = lax.dynamic_index_in_dim(here, me_x, 0, keepdims=False)
    other = lax.dynamic_index_in_dim(here, 1 - me_x, 0, keepdims=False)
    spans = jnp.concatenate([own, other])
    count = key_spans.shape[0]
    slots = jnp.arange(count, dtype=jnp.int32)
    rank = jnp.sum((key_spans[None, :] < key_spans[:, None]).astype(jnp.int32), axis=1)
    at_rank = rank[None, :] == slots[:, None]
    slot_of = jnp.sum(jnp.where(at_rank, slots[None, :], 0), axis=1)
    pos_of = jnp.sum(jnp.where(at_rank, key_spans[None, :], 0), axis=1)
    less = jnp.sum((key_spans[None, :] < spans[:, None]).astype(jnp.int32), axis=1)
    seen = jnp.sum((key_spans[None, :] <= spans[:, None]).astype(jnp.int32), axis=1)
    return jnp.concatenate([slot_of, pos_of, spans, less, seen])


def per_device(
    span_ids,
    hidden_in,
    queries,
    keys_in,
    values_in,
    attn_out,
    out_grad,
    log_norm,
    adapter,
    moment_first,
    moment_second,
):
    f32, low = jnp.float32, jnp.bfloat16
    z_count = lax.axis_size("ctx_0")
    dp_count = lax.axis_size("dp")
    width = adapter.shape[1]
    query_rows, grad_rows, input_rows = queries[0], out_grad[0], hidden_in[0]

    kv_rows = jnp.concatenate([keys_in[0], values_in[0]], axis=1)
    kv_all = lax.all_gather(kv_rows, "ctx_0", axis=0, tiled=True)

    query_other = swapped(query_rows)
    grad_other = swapped(grad_rows)
    products = grad_rows.astype(f32) * attn_out[0].astype(f32)
    delta = jnp.sum(products.reshape(ROWS, H, DH), axis=-1)
    own_stats = jnp.stack([stat_rows(log_norm[0]), stat_rows(delta)])
    stats = jnp.concatenate([own_stats, swapped(own_stats)], axis=2)
    stats = stats.reshape(2, 2 * KVH * ROWS // HALF, GROUP * HALF)
    table = span_tables(span_ids[0])
    prepared_rows = prepared(query_rows, grad_rows, query_other, grad_other)

    adapter_low = from_everyone(adapter.astype(low), "dp")
    adapter_low = jnp.transpose(adapter_low, (1, 0, 2)).reshape(adapter.shape[0], dp_count * width)
    mixed_down = lax.dot_general(
        adapter_low[:, :D], input_rows, (((1,), (1,)), ((), ())), preferred_element_type=f32
    ).astype(low)
    mixed_down = from_everyone(mixed_down, "ctx_0")
    mixed_down = jnp.transpose(mixed_down, (1, 0, 2)).reshape(adapter.shape[0], z_count * ROWS)

    prepared_rows, mixed_down, adapter_low = lax.optimization_barrier(
        (prepared_rows, mixed_down, adapter_low)
    )
    query_terms, kv_part = attention_terms(table, kv_all, prepared_rows, stats)
    kv_low = lax.psum_scatter(kv_part, "ctx_0", scatter_dimension=0, tiled=True)

    query_total = query_terms[:ROWS] + swapped(query_terms[ROWS:].astype(low)).astype(f32)
    query_grad = query_total.astype(low)

    up_terms = lax.dot_general(
        adapter_low[:, D:], kv_part, (((1,), (1,)), ((), ())), preferred_element_type=f32
    )
    up_terms = jnp.transpose(up_terms.reshape(adapter.shape[0], z_count, ROWS), (1, 0, 2))
    mixed_up = lax.all_to_all(up_terms, "ctx_0", 0, 0, tiled=True).sum(axis=0).astype(low)
    grad_up = jnp.dot(mixed_down, kv_part, preferred_element_type=f32)
    grad_down = jnp.dot(mixed_up, input_rows, preferred_element_type=f32)
    grad_partial = jnp.concatenate([grad_down, grad_up], axis=1).astype(low)
    pieces = jnp.transpose(grad_partial.reshape(adapter.shape[0], dp_count, width), (1, 0, 2))
    pieces = jnp.broadcast_to(pieces[:, None], (dp_count, 2, *adapter.shape))
    pieces = pieces.reshape(2 * dp_count, *adapter.shape)
    arrived = lax.all_to_all(pieces, ("dp", "ctx_1"), 0, 0, tiled=True)
    grad_shard = arrived.astype(f32).sum(axis=0)
    grad_shard = from_everyone(grad_shard.astype(low), "ctx_0").astype(f32).sum(axis=0)
    squares = from_everyone(jnp.sum(grad_shard * grad_shard), "dp").sum(axis=0)
    clip_factor = jnp.minimum(1.0, 1.0 / jnp.sqrt(squares + 1e-06))
    scaled = grad_shard * clip_factor
    moment_new = 0.9 * moment_first + 0.1 * scaled
    second_new = 0.999 * moment_second + 0.001 * scaled * scaled
    adapter_step = moment_new / BIAS_ONE / (jnp.sqrt(second_new / BIAS_TWO) + 1e-08)
    return (query_grad[None], kv_low[None], adapter_step)


def solution(mesh):
    torus = Mesh(mesh.devices.reshape(mesh.shape["dp"], -1, 2), ("dp", "ctx_0", "ctx_1"))
    placed = (
        P("dp", None),
        P("dp", CTX, None),
        P("dp", CTX, None),
        P("dp", CTX, None),
        P("dp", CTX, None),
        P("dp", CTX, None),
        P("dp", CTX, None),
        P("dp", CTX, None),
        P(None, "dp"),
        P(None, "dp"),
        P(None, "dp"),
    )
    return jax.shard_map(
        per_device,
        mesh=torus,
        in_specs=placed,
        out_specs=(P("dp", CTX, None), P("dp", CTX, None), P(None, "dp")),
        check_vma=False,
    )
```

```python
import jax
import jax.numpy as jnp
from jax import lax
from jax.experimental import pallas as pl
from jax.experimental.pallas import tpu as pltpu
from jax.sharding import Mesh
from jax.sharding import PartitionSpec as P

D = 4096
H = 16
KVH = 4
DH = 128
ROWS = 128
HALF = 64
GROUP = H // KVH
KEY_BLOCK = 256
SCALE = DH ** (-0.5)
CTX = ("ctx_0", "ctx_1")
PAIR = ((0, 1), (1, 0))


BIAS_ONE = 1.0 - 0.9**100.0
BIAS_TWO = 1.0 - 0.999**100.0


def attention_kernel(
    table_ref, kv_hbm, q_mine, g_mine, q_other, g_other, stat_ref,
    dq_mine, dq_other, dkv_hbm,
    raw_s, kv_s, dk_s, dv_s, dkv_s, q_s, g_s, qt_s, gt_s, dqt_s, raw_sem, in_sem, out_sem,
):
    n_blocks = kv_s.shape[0]
    n_spans = q_s.shape[0] // KVH
    per_block = KEY_BLOCK // HALF
    n_rows = GROUP * HALF
    value_at = KVH * DH
    pos_at = n_blocks * per_block
    span_at = 2 * pos_at
    less_at = span_at + n_spans
    seen_at = less_at + n_spans

    sources = (q_mine, g_mine, q_other, g_other)
    raw_copies = [pltpu.make_async_copy(source, raw_s.at[i], raw_sem.at[i]) for i, source in enumerate(sources)]
    for copy in raw_copies:
        copy.start()

    def span_in(rank):
        row = pl.multiple_of(table_ref[rank] * HALF, HALF)
        place = pl.multiple_of(lax.rem(rank, per_block) * HALF, HALF)
        return pltpu.make_async_copy(
            kv_hbm.at[pl.ds(row, HALF), :], kv_s.at[rank // per_block, pl.ds(place, HALF), :], in_sem.at[rank]
        )

    def span_out(rank):
        row = pl.multiple_of(table_ref[rank] * HALF, HALF)
        place = pl.multiple_of(lax.rem(rank, per_block) * HALF, HALF)
        return pltpu.make_async_copy(
            dkv_s.at[rank // per_block, pl.ds(place, HALF), :], dkv_hbm.at[pl.ds(row, HALF), :], out_sem.at[rank]
        )

    def start_in(rank, carry):
        span_in(rank).start()
        return carry

    lax.fori_loop(0, pos_at, start_in, 0)
    for copy in raw_copies:
        copy.wait()

    halves = ROWS // HALF
    for j in range(KVH):
        for s in range(n_spans):
            first = (s % halves) * HALF
            for kind, rows_out, cols_out in ((0, q_s, qt_s), (1, g_s, gt_s)):
                source = raw_s.at[2 * (s // halves) + kind]
                rows = jnp.concatenate(
                    [
                        source[first : first + HALF, (j * GROUP + g) * DH : (j * GROUP + g + 1) * DH]
                        for g in range(GROUP)
                    ],
                    axis=0,
                )
                rows_out[j * n_spans + s] = rows
                cols_out[j * n_spans + s] = rows.T
            dqt_s[j * n_spans + s] = jnp.zeros((DH, n_rows), jnp.float32)

    def key_cols(j):
        return slice(j * DH, (j + 1) * DH)

    def value_cols(j):
        return slice(value_at + j * DH, value_at + (j + 1) * DH)

    def heads(b, s, masked):
        if masked:
            lane = lax.broadcasted_iota(jnp.int32, (HALF, n_rows), 1)
            line = lax.broadcasted_iota(jnp.int32, (HALF, n_rows), 0)
            ahead = line - lax.rem(lane, HALF)
            visible = jnp.concatenate(
                [
                    ahead <= (table_ref[span_at + s] - table_ref[pos_at + b * per_block + i]) * HALF
                    for i in range(per_block)
                ],
                axis=0,
            )
        def front(j):
            n = j * n_spans + s
            scores = jnp.dot(kv_s[b, :, key_cols(j)], qt_s[n], preferred_element_type=jnp.float32)
            d_weights = jnp.dot(kv_s[b, :, value_cols(j)], gt_s[n], preferred_element_type=jnp.float32)
            return scores, d_weights

        def middle(j, scores, d_weights):
            n = j * n_spans + s
            weights = jnp.exp(scores * SCALE - stat_ref[0, pl.ds(n, 1), :])
            if masked:
                weights = jnp.where(visible, weights, 0.0)
            d_scores = (weights * (d_weights - stat_ref[1, pl.ds(n, 1), :])).astype(jnp.bfloat16)
            return weights.astype(jnp.bfloat16), d_scores

        def back(j, weights_low, d_scores):
            n = j * n_spans + s
            dv_s[j] += jnp.dot(weights_low, g_s[n], preferred_element_type=jnp.float32)
            dk_s[j] += jnp.dot(d_scores, q_s[n], preferred_element_type=jnp.float32)
            dqt_s[n] += lax.dot_general(
                kv_s[b, :, key_cols(j)], d_scores, (((0,), (0,)), ((), ())), preferred_element_type=jnp.float32
            )

        fronts = front(0)
        for j in range(KVH):
            middles = middle(j, *fronts)
            if j + 1 < KVH:
                fronts = front(j + 1)
            back(j, *middles)

    def block(b, carry):
        for i in range(per_block):
            span_in(b * per_block + i).wait()
        for j in range(KVH):
            dk_s[j] = jnp.zeros((KEY_BLOCK, DH), jnp.float32)
            dv_s[j] = jnp.zeros((KEY_BLOCK, DH), jnp.float32)

        def query_span(s, c):
            whole = table_ref[less_at + s] >= (b + 1) * per_block

            @pl.when(whole)
            def _():
                heads(b, s, False)

            @pl.when(jnp.logical_and(jnp.logical_not(whole), table_ref[seen_at + s] > b * per_block))
            def _():
                heads(b, s, True)

            return c

        lax.fori_loop(0, n_spans, query_span, 0)
        for j in range(KVH):
            dkv_s[b, :, key_cols(j)] = (dk_s[j] * SCALE).astype(jnp.bfloat16)
            dkv_s[b, :, value_cols(j)] = dv_s[j].astype(jnp.bfloat16)
        for i in range(per_block):
            span_out(b * per_block + i).start()
        return carry

    lax.fori_loop(0, n_blocks, block, 0)

    for j in range(KVH):
        for s in range(n_spans):
            total = (dqt_s[j * n_spans + s] * SCALE).T
            for g in range(GROUP):
                cols = slice((j * GROUP + g) * DH, (j * GROUP + g + 1) * DH)
                first = (s % halves) * HALF
                out = (dq_mine, dq_other)[s // halves]
                out[first : first + HALF, cols] = total[g * HALF : (g + 1) * HALF].astype(out.dtype)

    def finish_out(rank, carry):
        span_out(rank).wait()
        return carry

    lax.fori_loop(0, pos_at, finish_out, 0)


def attention_terms(table, kv, q_mine, g_mine, q_other, g_other, stats):
    length = kv.shape[0]
    n_blocks = length // KEY_BLOCK
    n_slots = length // HALF
    n_spans = 2 * ROWS // HALF
    count = KVH * n_spans
    smem = pl.BlockSpec(memory_space=pltpu.SMEM)
    vmem = pl.BlockSpec(memory_space=pltpu.VMEM)
    hbm = pl.BlockSpec(memory_space=pltpu.HBM)
    bf, f32 = jnp.bfloat16, jnp.float32
    return pl.pallas_call(
        attention_kernel,
        out_shape=(
            jax.ShapeDtypeStruct(q_mine.shape, f32),
            jax.ShapeDtypeStruct(q_mine.shape, bf),
            jax.ShapeDtypeStruct(kv.shape, bf),
        ),
        in_specs=[smem] + [hbm] * 5 + [vmem],
        out_specs=(vmem, vmem, hbm),
        scratch_shapes=[
            pltpu.VMEM((4, *q_mine.shape), bf),
            pltpu.VMEM((n_blocks, KEY_BLOCK, kv.shape[1]), bf),
            pltpu.VMEM((KVH, KEY_BLOCK, DH), f32),
            pltpu.VMEM((KVH, KEY_BLOCK, DH), f32),
            pltpu.VMEM((n_blocks, KEY_BLOCK, kv.shape[1]), bf),
            pltpu.VMEM((count, GROUP * HALF, DH), bf),
            pltpu.VMEM((count, GROUP * HALF, DH), bf),
            pltpu.VMEM((count, DH, GROUP * HALF), bf),
            pltpu.VMEM((count, DH, GROUP * HALF), bf),
            pltpu.VMEM((count, DH, GROUP * HALF), f32),
            pltpu.SemaphoreType.DMA((4,)),
            pltpu.SemaphoreType.DMA((n_slots,)),
            pltpu.SemaphoreType.DMA((n_slots,)),
        ],
        compiler_params=pltpu.CompilerParams(vmem_limit_bytes=52 * 1024 * 1024),
    )(table, kv, q_mine, g_mine, q_other, g_other, stats)


def from_everyone(shard, axis):
    count = lax.axis_size(axis)
    return lax.all_to_all(
        jnp.broadcast_to(shard[None], (count, *shard.shape)), axis, 0, 0, tiled=True
    )


def swapped(block):
    return lax.ppermute(block, "ctx_1", PAIR)


def stat_rows(stats):
    tall = stats.reshape(ROWS // HALF, HALF, KVH, GROUP)
    return jnp.transpose(tall, (2, 0, 3, 1)).reshape(KVH, ROWS // HALF, GROUP * HALF)


def span_tables(span_ids):
    me_x = lax.axis_index("ctx_1")
    places = span_ids.reshape(lax.axis_size("ctx_0"), 2, ROWS // HALF)
    key_spans = lax.dynamic_index_in_dim(places, me_x, 1, keepdims=False).reshape(-1)
    here = lax.dynamic_index_in_dim(places, lax.axis_index("ctx_0"), 0, keepdims=False)
    own = lax.dynamic_index_in_dim(here, me_x, 0, keepdims=False)
    other = lax.dynamic_index_in_dim(here, 1 - me_x, 0, keepdims=False)
    spans = jnp.concatenate([own, other])
    count = key_spans.shape[0]
    slots = jnp.arange(count, dtype=jnp.int32)
    rank = jnp.sum((key_spans[None, :] < key_spans[:, None]).astype(jnp.int32), axis=1)
    at_rank = rank[None, :] == slots[:, None]
    slot_of = jnp.sum(jnp.where(at_rank, slots[None, :], 0), axis=1)
    pos_of = jnp.sum(jnp.where(at_rank, key_spans[None, :], 0), axis=1)
    less = jnp.sum((key_spans[None, :] < spans[:, None]).astype(jnp.int32), axis=1)
    seen = jnp.sum((key_spans[None, :] <= spans[:, None]).astype(jnp.int32), axis=1)
    return jnp.concatenate([slot_of, pos_of, spans, less, seen])


def per_device(
    span_ids,
    hidden_in,
    queries,
    keys_in,
    values_in,
    attn_out,
    out_grad,
    log_norm,
    adapter,
    moment_first,
    moment_second,
):
    f32, low = jnp.float32, jnp.bfloat16
    z_count = lax.axis_size("ctx_0")
    dp_count = lax.axis_size("dp")
    width = adapter.shape[1]
    query_rows, grad_rows, input_rows = queries[0], out_grad[0], hidden_in[0]

    kv_rows = jnp.concatenate([keys_in[0], values_in[0]], axis=1)
    kv_all = lax.all_gather(kv_rows, "ctx_0", axis=0, tiled=True)

    query_other = swapped(query_rows)
    grad_other = swapped(grad_rows)
    products = grad_rows.astype(f32) * attn_out[0].astype(f32)
    delta = jnp.sum(products.reshape(ROWS, H, DH), axis=-1)
    own_stats = jnp.stack([stat_rows(log_norm[0]), stat_rows(delta)])
    stats = jnp.concatenate([own_stats, swapped(own_stats)], axis=2)
    stats = stats.reshape(2, 2 * KVH * ROWS // HALF, GROUP * HALF)
    table = span_tables(span_ids[0])

    adapter_low = from_everyone(adapter.astype(low), "dp")
    adapter_low = jnp.transpose(adapter_low, (1, 0, 2)).reshape(adapter.shape[0], dp_count * width)
    mixed_down = lax.dot_general(
        adapter_low[:, :D], input_rows, (((1,), (1,)), ((), ())), preferred_element_type=f32
    ).astype(low)
    mixed_down = from_everyone(mixed_down, "ctx_0")
    mixed_down = jnp.transpose(mixed_down, (1, 0, 2)).reshape(adapter.shape[0], z_count * ROWS)

    stats, mixed_down, adapter_low = lax.optimization_barrier((stats, mixed_down, adapter_low))
    query_terms, other_terms, kv_part = attention_terms(
        table, kv_all, query_rows, grad_rows, query_other, grad_other, stats
    )
    kv_low = lax.psum_scatter(kv_part, "ctx_0", scatter_dimension=0, tiled=True)

    query_grad = (query_terms + swapped(other_terms).astype(f32)).astype(low)

    up_terms = lax.dot_general(
        adapter_low[:, D:], kv_part, (((1,), (1,)), ((), ())), preferred_element_type=f32
    )
    up_terms = jnp.transpose(up_terms.reshape(adapter.shape[0], z_count, ROWS), (1, 0, 2))
    mixed_up = lax.all_to_all(up_terms, "ctx_0", 0, 0, tiled=True).sum(axis=0).astype(low)
    grad_up = jnp.dot(mixed_down, kv_part, preferred_element_type=f32)
    grad_down = jnp.dot(mixed_up, input_rows, preferred_element_type=f32)
    grad_partial = jnp.concatenate([grad_down, grad_up], axis=1).astype(low)
    pieces = jnp.transpose(grad_partial.reshape(adapter.shape[0], dp_count, width), (1, 0, 2))
    pieces = jnp.broadcast_to(pieces[:, None], (dp_count, 2, *adapter.shape))
    pieces = pieces.reshape(2 * dp_count, *adapter.shape)
    arrived = lax.all_to_all(pieces, ("dp", "ctx_1"), 0, 0, tiled=True)
    grad_shard = arrived.astype(f32).sum(axis=0)
    grad_shard = from_everyone(grad_shard.astype(low), "ctx_0").astype(f32).sum(axis=0)
    squares = from_everyone(jnp.sum(grad_shard * grad_shard), "dp").sum(axis=0)
    clip_factor = jnp.minimum(1.0, 1.0 / jnp.sqrt(squares + 1e-06))
    scaled = grad_shard * clip_factor
    moment_new = 0.9 * moment_first + 0.1 * scaled
    second_new = 0.999 * moment_second + 0.001 * scaled * scaled
    adapter_step = moment_new / BIAS_ONE / (jnp.sqrt(second_new / BIAS_TWO) + 1e-08)
    return (query_grad[None], kv_low[None], adapter_step)


def solution(mesh):
    torus = Mesh(mesh.devices.reshape(mesh.shape["dp"], -1, 2), ("dp", "ctx_0", "ctx_1"))
    placed = (
        P("dp", None),
        P("dp", CTX, None),
        P("dp", CTX, None),
        P("dp", CTX, None),
        P("dp", CTX, None),
        P("dp", CTX, None),
        P("dp", CTX, None),
        P("dp", CTX, None),
        P(None, "dp"),
        P(None, "dp"),
        P(None, "dp"),
    )
    return jax.shard_map(
        per_device,
        mesh=torus,
        in_specs=placed,
        out_specs=(P("dp", CTX, None), P("dp", CTX, None), P(None, "dp")),
        check_vma=False,
    )
```

```python
import jax
import jax.numpy as jnp
from jax import lax
from jax.experimental import pallas as pl
from jax.experimental.pallas import tpu as pltpu
from jax.sharding import Mesh
from jax.sharding import PartitionSpec as P

D = 4096
H = 16
KVH = 4
DH = 128
ROWS = 128
HALF = 64
GROUP = H // KVH
KEY_BLOCK = 256
SCALE = DH ** (-0.5)
CTX = ("ctx_0", "ctx_1")
PAIR = ((0, 1), (1, 0))


BIAS_ONE = 1.0 - 0.9**100.0
BIAS_TWO = 1.0 - 0.999**100.0


def attention_kernel(
    table_ref, kv_hbm, q_mine, g_mine, q_other, g_other, stat_ref,
    dq_mine, dq_other, dkv_hbm,
    raw_s, kv_s, dk_s, dv_s, dkv_s, q_s, g_s, qt_s, gt_s, dqt_s, raw_sem, in_sem, out_sem,
):
    n_blocks = kv_s.shape[0]
    n_spans = q_s.shape[0] // KVH
    per_block = KEY_BLOCK // HALF
    n_rows = GROUP * HALF
    value_at = KVH * DH
    pos_at = n_blocks * per_block
    span_at = 2 * pos_at
    less_at = span_at + n_spans
    seen_at = less_at + n_spans

    sources = (q_mine, g_mine, q_other, g_other)
    raw_copies = [pltpu.make_async_copy(source, raw_s.at[i], raw_sem.at[i]) for i, source in enumerate(sources)]
    for copy in raw_copies:
        copy.start()

    def span_in(rank):
        row = pl.multiple_of(table_ref[rank] * HALF, HALF)
        place = pl.multiple_of(lax.rem(rank, per_block) * HALF, HALF)
        return pltpu.make_async_copy(
            kv_hbm.at[pl.ds(row, HALF), :], kv_s.at[rank // per_block, pl.ds(place, HALF), :], in_sem.at[rank]
        )

    def span_out(rank):
        row = pl.multiple_of(table_ref[rank] * HALF, HALF)
        place = pl.multiple_of(lax.rem(rank, per_block) * HALF, HALF)
        return pltpu.make_async_copy(
            dkv_s.at[rank // per_block, pl.ds(place, HALF), :], dkv_hbm.at[pl.ds(row, HALF), :], out_sem.at[rank]
        )

    def block_at(turn):
        return jnp.where(turn == 0, 0, n_blocks - turn)

    def start_in(turn, carry):
        for i in range(per_block):
            span_in(block_at(turn) * per_block + i).start()
        return carry

    lax.fori_loop(0, n_blocks, start_in, 0)
    for copy in raw_copies:
        copy.wait()

    halves = ROWS // HALF
    for j in range(KVH):
        for s in range(n_spans):
            first = (s % halves) * HALF
            for kind, rows_out, cols_out in ((0, q_s, qt_s), (1, g_s, gt_s)):
                source = raw_s.at[2 * (s // halves) + kind]
                rows = jnp.concatenate(
                    [
                        source[first : first + HALF, (j * GROUP + g) * DH : (j * GROUP + g + 1) * DH]
                        for g in range(GROUP)
                    ],
                    axis=0,
                )
                rows_out[j * n_spans + s] = rows
                cols_out[j * n_spans + s] = rows.T
            dqt_s[j * n_spans + s] = jnp.zeros((DH, n_rows), jnp.float32)

    def key_cols(j):
        return slice(j * DH, (j + 1) * DH)

    def value_cols(j):
        return slice(value_at + j * DH, value_at + (j + 1) * DH)

    def heads(b, s, masked, rows=KEY_BLOCK):
        if masked:
            lane = lax.broadcasted_iota(jnp.int32, (HALF, n_rows), 1)
            line = lax.broadcasted_iota(jnp.int32, (HALF, n_rows), 0)
            ahead = line - lax.rem(lane, HALF)
            visible = jnp.concatenate(
                [
                    ahead <= (table_ref[span_at + s] - table_ref[pos_at + b * per_block + i]) * HALF
                    for i in range(rows // HALF)
                ],
                axis=0,
            )
        def front(j):
            n = j * n_spans + s
            scores = jnp.dot(kv_s[b, :rows, key_cols(j)], qt_s[n], preferred_element_type=jnp.float32)
            d_weights = jnp.dot(kv_s[b, :rows, value_cols(j)], gt_s[n], preferred_element_type=jnp.float32)
            return scores, d_weights

        def middle(j, scores, d_weights):
            n = j * n_spans + s
            weights = jnp.exp(scores * SCALE - stat_ref[0, pl.ds(n, 1), :])
            if masked:
                weights = jnp.where(visible, weights, 0.0)
            d_scores = (weights * (d_weights - stat_ref[1, pl.ds(n, 1), :])).astype(jnp.bfloat16)
            return weights.astype(jnp.bfloat16), d_scores

        def back(j, weights_low, d_scores):
            n = j * n_spans + s
            dv_s[j, :rows] += jnp.dot(weights_low, g_s[n], preferred_element_type=jnp.float32)
            dk_s[j, :rows] += jnp.dot(d_scores, q_s[n], preferred_element_type=jnp.float32)
            dqt_s[n] += lax.dot_general(
                kv_s[b, :rows, key_cols(j)], d_scores, (((0,), (0,)), ((), ())), preferred_element_type=jnp.float32
            )

        fronts = front(0)
        for j in range(KVH):
            middles = middle(j, *fronts)
            if j + 1 < KVH:
                fronts = front(j + 1)
            back(j, *middles)

    def block(turn, carry):
        b = block_at(turn)
        for i in range(per_block):
            span_in(b * per_block + i).wait()
        for j in range(KVH):
            dk_s[j] = jnp.zeros((KEY_BLOCK, DH), jnp.float32)
            dv_s[j] = jnp.zeros((KEY_BLOCK, DH), jnp.float32)

        def query_span(s, c):
            whole = table_ref[less_at + s] >= (b + 1) * per_block

            @pl.when(whole)
            def _():
                heads(b, s, False)

            seen = table_ref[seen_at + s] - b * per_block

            @pl.when(jnp.logical_and(jnp.logical_not(whole), seen > per_block // 2))
            def _():
                heads(b, s, True)

            @pl.when(jnp.logical_and(seen > 0, seen <= per_block // 2))
            def _():
                heads(b, s, True, KEY_BLOCK // 2)

            return c

        lax.fori_loop(0, n_spans, query_span, 0)
        for j in range(KVH):
            dkv_s[b, :, key_cols(j)] = (dk_s[j] * SCALE).astype(jnp.bfloat16)
            dkv_s[b, :, value_cols(j)] = dv_s[j].astype(jnp.bfloat16)
        for i in range(per_block):
            span_out(b * per_block + i).start()
        return carry

    lax.fori_loop(0, n_blocks, block, 0)

    for j in range(KVH):
        for s in range(n_spans):
            total = (dqt_s[j * n_spans + s] * SCALE).T
            for g in range(GROUP):
                cols = slice((j * GROUP + g) * DH, (j * GROUP + g + 1) * DH)
                first = (s % halves) * HALF
                out = (dq_mine, dq_other)[s // halves]
                out[first : first + HALF, cols] = total[g * HALF : (g + 1) * HALF].astype(out.dtype)

    def finish_out(rank, carry):
        span_out(rank).wait()
        return carry

    lax.fori_loop(0, pos_at, finish_out, 0)


def attention_terms(table, kv, q_mine, g_mine, q_other, g_other, stats):
    length = kv.shape[0]
    n_blocks = length // KEY_BLOCK
    n_slots = length // HALF
    n_spans = 2 * ROWS // HALF
    count = KVH * n_spans
    smem = pl.BlockSpec(memory_space=pltpu.SMEM)
    vmem = pl.BlockSpec(memory_space=pltpu.VMEM)
    hbm = pl.BlockSpec(memory_space=pltpu.HBM)
    bf, f32 = jnp.bfloat16, jnp.float32
    return pl.pallas_call(
        attention_kernel,
        out_shape=(
            jax.ShapeDtypeStruct(q_mine.shape, f32),
            jax.ShapeDtypeStruct(q_mine.shape, bf),
            jax.ShapeDtypeStruct(kv.shape, bf),
        ),
        in_specs=[smem] + [hbm] * 5 + [vmem],
        out_specs=(vmem, vmem, hbm),
        scratch_shapes=[
            pltpu.VMEM((4, *q_mine.shape), bf),
            pltpu.VMEM((n_blocks, KEY_BLOCK, kv.shape[1]), bf),
            pltpu.VMEM((KVH, KEY_BLOCK, DH), f32),
            pltpu.VMEM((KVH, KEY_BLOCK, DH), f32),
            pltpu.VMEM((n_blocks, KEY_BLOCK, kv.shape[1]), bf),
            pltpu.VMEM((count, GROUP * HALF, DH), bf),
            pltpu.VMEM((count, GROUP * HALF, DH), bf),
            pltpu.VMEM((count, DH, GROUP * HALF), bf),
            pltpu.VMEM((count, DH, GROUP * HALF), bf),
            pltpu.VMEM((count, DH, GROUP * HALF), f32),
            pltpu.SemaphoreType.DMA((4,)),
            pltpu.SemaphoreType.DMA((n_slots,)),
            pltpu.SemaphoreType.DMA((n_slots,)),
        ],
        compiler_params=pltpu.CompilerParams(vmem_limit_bytes=52 * 1024 * 1024),
    )(table, kv, q_mine, g_mine, q_other, g_other, stats)


def from_everyone(shard, axis):
    count = lax.axis_size(axis)
    return lax.all_to_all(
        jnp.broadcast_to(shard[None], (count, *shard.shape)), axis, 0, 0, tiled=True
    )


def swapped(block):
    return lax.ppermute(block, "ctx_1", PAIR)


def stat_rows(stats):
    tall = stats.reshape(ROWS // HALF, HALF, KVH, GROUP)
    return jnp.transpose(tall, (2, 0, 3, 1)).reshape(KVH, ROWS // HALF, GROUP * HALF)


def span_tables(span_ids):
    me_x = lax.axis_index("ctx_1")
    places = span_ids.reshape(lax.axis_size("ctx_0"), 2, ROWS // HALF)
    key_spans = lax.dynamic_index_in_dim(places, me_x, 1, keepdims=False).reshape(-1)
    here = lax.dynamic_index_in_dim(places, lax.axis_index("ctx_0"), 0, keepdims=False)
    own = lax.dynamic_index_in_dim(here, me_x, 0, keepdims=False)
    other = lax.dynamic_index_in_dim(here, 1 - me_x, 0, keepdims=False)
    spans = jnp.concatenate([own, other])
    count = key_spans.shape[0]
    slots = jnp.arange(count, dtype=jnp.int32)
    rank = jnp.sum((key_spans[None, :] < key_spans[:, None]).astype(jnp.int32), axis=1)
    at_rank = rank[None, :] == slots[:, None]
    slot_of = jnp.sum(jnp.where(at_rank, slots[None, :], 0), axis=1)
    pos_of = jnp.sum(jnp.where(at_rank, key_spans[None, :], 0), axis=1)
    less = jnp.sum((key_spans[None, :] < spans[:, None]).astype(jnp.int32), axis=1)
    seen = jnp.sum((key_spans[None, :] <= spans[:, None]).astype(jnp.int32), axis=1)
    return jnp.concatenate([slot_of, pos_of, spans, less, seen])


def per_device(
    span_ids,
    hidden_in,
    queries,
    keys_in,
    values_in,
    attn_out,
    out_grad,
    log_norm,
    adapter,
    moment_first,
    moment_second,
):
    f32, low = jnp.float32, jnp.bfloat16
    z_count = lax.axis_size("ctx_0")
    dp_count = lax.axis_size("dp")
    width = adapter.shape[1]
    query_rows, grad_rows, input_rows = queries[0], out_grad[0], hidden_in[0]

    kv_rows = jnp.concatenate([keys_in[0], values_in[0]], axis=1)
    kv_all = lax.all_gather(kv_rows, "ctx_0", axis=0, tiled=True)

    query_other = swapped(query_rows)
    grad_other = swapped(grad_rows)
    products = grad_rows.astype(f32) * attn_out[0].astype(f32)
    delta = jnp.sum(products.reshape(ROWS, H, DH), axis=-1)
    own_stats = jnp.stack([stat_rows(log_norm[0]), stat_rows(delta)])
    stats = jnp.concatenate([own_stats, swapped(own_stats)], axis=2)
    stats = stats.reshape(2, 2 * KVH * ROWS // HALF, GROUP * HALF)
    table = span_tables(span_ids[0])

    adapter_low = from_everyone(adapter.astype(low), "dp")
    adapter_low = jnp.transpose(adapter_low, (1, 0, 2)).reshape(adapter.shape[0], dp_count * width)
    mixed_down = lax.dot_general(
        adapter_low[:, :D], input_rows, (((1,), (1,)), ((), ())), preferred_element_type=f32
    ).astype(low)
    mixed_down = from_everyone(mixed_down, "ctx_0")
    mixed_down = jnp.transpose(mixed_down, (1, 0, 2)).reshape(adapter.shape[0], z_count * ROWS)

    stats, mixed_down, adapter_low = lax.optimization_barrier((stats, mixed_down, adapter_low))
    query_terms, other_terms, kv_part = attention_terms(
        table, kv_all, query_rows, grad_rows, query_other, grad_other, stats
    )
    kv_low = lax.psum_scatter(kv_part, "ctx_0", scatter_dimension=0, tiled=True)

    query_grad = (query_terms + swapped(other_terms).astype(f32)).astype(low)

    up_terms = lax.dot_general(
        adapter_low[:, D:], kv_part, (((1,), (1,)), ((), ())), preferred_element_type=f32
    )
    up_terms = jnp.transpose(up_terms.reshape(adapter.shape[0], z_count, ROWS), (1, 0, 2))
    mixed_up = lax.all_to_all(up_terms, "ctx_0", 0, 0, tiled=True).sum(axis=0).astype(low)
    grad_up = jnp.dot(mixed_down, kv_part, preferred_element_type=f32)
    grad_down = jnp.dot(mixed_up, input_rows, preferred_element_type=f32)
    grad_partial = jnp.concatenate([grad_down, grad_up], axis=1).astype(low)
    pieces = jnp.transpose(grad_partial.reshape(adapter.shape[0], dp_count, width), (1, 0, 2))
    pieces = jnp.broadcast_to(pieces[:, None], (dp_count, 2, *adapter.shape))
    pieces = pieces.reshape(2 * dp_count, *adapter.shape)
    arrived = lax.all_to_all(pieces, ("dp", "ctx_1"), 0, 0, tiled=True)
    grad_shard = arrived.astype(f32).sum(axis=0)
    grad_shard = from_everyone(grad_shard.astype(low), "ctx_0").astype(f32).sum(axis=0)
    squares = from_everyone(jnp.sum(grad_shard * grad_shard), "dp").sum(axis=0)
    clip_factor = jnp.minimum(1.0, 1.0 / jnp.sqrt(squares + 1e-06))
    scaled = grad_shard * clip_factor
    moment_new = 0.9 * moment_first + 0.1 * scaled
    second_new = 0.999 * moment_second + 0.001 * scaled * scaled
    adapter_step = moment_new / BIAS_ONE / (jnp.sqrt(second_new / BIAS_TWO) + 1e-08)
    return (query_grad[None], kv_low[None], adapter_step)


def solution(mesh):
    torus = Mesh(mesh.devices.reshape(mesh.shape["dp"], -1, 2), ("dp", "ctx_0", "ctx_1"))
    placed = (
        P("dp", None),
        P("dp", CTX, None),
        P("dp", CTX, None),
        P("dp", CTX, None),
        P("dp", CTX, None),
        P("dp", CTX, None),
        P("dp", CTX, None),
        P("dp", CTX, None),
        P(None, "dp"),
        P(None, "dp"),
        P(None, "dp"),
    )
    return jax.shard_map(
        per_device,
        mesh=torus,
        in_specs=placed,
        out_specs=(P("dp", CTX, None), P("dp", CTX, None), P(None, "dp")),
        check_vma=False,
    )
```
